32 devices in a mesh: img: 8 (over z, core), ep: 4 (over y, x).
Axes of the slice: x: 2, y: 2, z: 4, core: 2. Of those that a mesh axis runs over, the one named last changes fastest.
Arguments:
- tokens: bfloat16 [1024, 8, 384], P('ep', 'img'), may hold values from -6 to 6
- cotangent: bfloat16 [1024, 8, 384], P('ep', 'img'), may hold values from -6 to 6
- valid: int32 [1024, 8], P(None, 'img'), may hold values from 0 to 1, as said below
- task_ids: int32 [8], P('img'), may hold values from 0 to 1
- top_counts: int32 [2], replicated, may hold values from 1 to 4
- expert_ids: int32 [1024, 8, 4], P('ep', 'img'), may hold values from 0 to 15, all different within a row
- gains: bfloat16 [2, 384], P(None, 'ep'), may hold values from 0.25 to 1.75
- shifts: bfloat16 [2, 384], P(None, 'ep'), may hold values from -1.5 to 1.5
- qkv_weight: bfloat16 [384, 1152], P('img', 'ep'), may hold values from -0.3125 to 0.3125
- out_weight: bfloat16 [384, 384], P('img', 'ep'), may hold values from -1.25 to 1.25
- router_weight: bfloat16 [2, 384, 16], P(None, 'img', 'ep'), may hold values from -0.625 to 0.625
- w_in: bfloat16 [16, 384, 1536], P('ep'), may hold values from -0.3125 to 0.3125
- w_out: bfloat16 [16, 1536, 384], P('ep'), may hold values from -0.625 to 0.625
Outputs:
- output: bfloat16 [1024, 8, 384], P('ep', 'img')
- grad_tokens: float32 [1024, 8, 384], P('ep', 'img')
- grad_gains: float32 [2, 384], P(None, 'ep')
- grad_shifts: float32 [2, 384], P(None, 'ep')
- grad_qkv: float32 [384, 1152], P('img', 'ep')
- grad_out: float32 [384, 384], P('img', 'ep')
- grad_router: float32 [2, 384, 16], P(None, 'img', 'ep')
- grad_w_in: float32 [16, 384, 1536], P('ep')
- grad_w_out: float32 [16, 1536, 384], P('ep')
The draws below stay inside these ranges and needn't reach their ends.
Inputs may be any that keep to these rules, and one draw needn't show every extreme that they name: Cell g of an image lies in grid row g // 32 and column g % 32; an image's valid cells are those in its first h rows and first w columns, h and w each from 8 to 32.
All inputs are finite; a program needn't handle non-finite values.
Results may differ from the reference program's by a relative error of at most 0.018.
Values may be sent and summed in bfloat16 or wider, within the bound.
No kernel may reach another device: no remote copies, remote signals or barrier semaphores. Data moves between devices by JAX's collectives and lax.ppermute only.
A program may use at most 128 MiB of HBM per device.

```python
import jax
import jax.numpy as jnp
from jax import lax

D = 384
FF = 1536
HEADS = 6
HD = 64
EXPERTS = 16
TASKS = 2
TOP_MAX = 4
SIDE = 32
GRID = 1024
IMG_GROUP = 1
SEG_ROWS = 256
IMAGES = 8
CAPACITY = 32
N_IMG = 8
N_EP = 4


def draw_valid(key, part):
    key_rows = jax.random.fold_in(key, 11)
    key_cols = jax.random.fold_in(key, 12)
    heights = jax.random.randint(key_rows, (IMAGES,), SIDE // 4, SIDE + 1)
    widths = jax.random.randint(key_cols, (IMAGES,), SIDE // 4, SIDE + 1)
    cells = jnp.arange(GRID, dtype=jnp.int32)
    grid_row = cells // SIDE
    grid_col = cells % SIDE
    inside = (grid_row[:, None] < heights[None, :]) & (grid_col[:, None] < widths[None, :])
    return inside.astype(jnp.int32)


def draw_top_counts(key, part):
    key_counts = jax.random.fold_in(key, 21)
    key_pick = jax.random.fold_in(key, 22)
    counts = jax.random.randint(key_counts, (TASKS,), 1, TOP_MAX + 1)
    chosen_task = jax.random.randint(key_pick, (), 0, TASKS)
    return jnp.where(jnp.arange(TASKS, dtype=jnp.int32) == chosen_task, TOP_MAX, counts).astype(jnp.int32)


def set_ends(entries, rng, low, high):
    longest = entries.shape.index(max(entries.shape))
    spots = []
    for shift in (0, 1):
        where = [jax.random.randint(jax.random.fold_in(rng, axis), (), 0, length) for axis, length in enumerate(entries.shape)]
        where[longest] = (where[longest] + shift) % entries.shape[longest]
        spots.append(tuple(where))
    return entries.at[spots[0]].set(low).at[spots[1]].set(high)


def levels(stream_key, shape, cuts, smallest, high):
    level = 1.0
    for axis_at, shards_of in cuts:
        steps = jax.random.uniform(jax.random.fold_in(jax.random.fold_in(stream_key, 6), axis_at), (shards_of,), jnp.float32, smallest / len(cuts), high / len(cuts))
        level = level * jnp.repeat(jnp.exp(steps), shape[axis_at] // shards_of).reshape((-1,) + (1,) * (len(shape) - 1 - axis_at))
    return level


def choose_distinct(own_key, rows, count, top, lift):
    sequence = jax.random.permutation(jax.random.fold_in(own_key, 1), count)
    pull = sequence
    for power in range(3):
        pull = pull * pull // count
    pull = pull * lift // count
    lots = jax.random.randint(jax.random.fold_in(own_key, 2), (rows, count), 0, 4096) + pull
    holders = jax.random.permutation(jax.random.fold_in(own_key, 3), rows)[jnp.arange(count) % rows]
    lots = jnp.where(jnp.arange(rows)[:, None] == holders[None, :], 1 << 14, lots)
    priority = lots * count + jnp.arange(count)
    return lax.top_k(priority.astype(jnp.int32), top)[1].astype(jnp.int32)


def noise(rng, extent, scale, limit, cuts=(), held_as=jnp.bfloat16):
    loudness = levels(rng, extent, cuts, -0.22, 0.18) if cuts else 1.0
    values = jax.random.normal(rng, extent, jnp.float32) * scale * loudness
    return jnp.minimum(jnp.maximum(values, -limit), limit).astype(held_as)


def setup_inputs(seed: int = 0) -> dict:
    splits = jax.random.split(jax.random.key(seed), 14)
    return {
        "tokens": noise(splits[0], (GRID, IMAGES, D), 1.0, 6.0, ((0, 4), (1, 8))),
        "cotangent": noise(splits[1], (GRID, IMAGES, D), 1.0, 6.0, ((0, 4), (1, 8))),
        "valid": draw_valid(jax.random.fold_in(splits[13], 71), 0),
        "task_ids": set_ends(jax.random.randint(splits[3], (IMAGES,), 0, TASKS), jax.random.fold_in(splits[3], 1), 0, TASKS - 1).astype(jnp.int32),
        "top_counts": draw_top_counts(jax.random.fold_in(splits[13], 71), 0),
        "expert_ids": choose_distinct(splits[5], GRID * IMAGES, EXPERTS, TOP_MAX, 4096).reshape((GRID, IMAGES, TOP_MAX)),
        "gains": jnp.clip(1.0 + 0.15 * jax.random.normal(splits[6], (2, D), jnp.float32), 0.25, 1.75).astype(jnp.bfloat16),
        "shifts": noise(splits[7], (2, D), 0.3, 1.5, ((1, 4),)),
        "qkv_weight": noise(splits[8], (D, 3 * D), D ** -0.5, 0.3125, ((0, 8), (1, 4))),
        "out_weight": noise(splits[9], (D, D), (D // 16) ** -0.5, 1.25, ((0, 8), (1, 4))),
        "router_weight": noise(splits[10], (TASKS, D, EXPERTS), (D // 4) ** -0.5, 0.625, ((1, 8), (2, 4))),
        "w_in": noise(splits[11], (EXPERTS, D, FF), D ** -0.5, 0.3125, ((0, 4),)),
        "w_out": noise(splits[12], (EXPERTS, FF, D), (FF // 16) ** -0.5, 0.625, ((0, 4),)),
    }


norm_eps = 1e-06
highest = lax.Precision.HIGHEST
masked_score = -1e+30

@jax.custom_vjp
def low(v):
    return lax.optimization_barrier(v.astype(jnp.bfloat16)).astype(jnp.float32)

@jax.custom_vjp
def low_back(v):
    return v

def low_keep(v):
    return (low(v), None)

def low_pass(kept, grad):
    return (grad,)

def back_keep(v):
    return (v, None)

def back_low(kept, grad):
    return (low(grad),)
low.defvjp(low_keep, low_pass)
low_back.defvjp(back_keep, back_low)

def layer_norm(values, gain, shift):
    centre = lax.optimization_barrier(jnp.mean(values, axis=-1, keepdims=True))
    centred = values - centre
    spread = lax.optimization_barrier(jnp.mean(centred * centred, axis=-1, keepdims=True))
    return centred * lax.rsqrt(spread + norm_eps) * gain + shift

def softmax_rows(scores):
    row_max = lax.optimization_barrier(jnp.max(scores, axis=-1, keepdims=True))
    exp_terms = jnp.exp(scores - row_max)
    return exp_terms / lax.optimization_barrier(jnp.sum(exp_terms, axis=-1, keepdims=True))

def route_slots(choices, used_mask):
    row_count, choice_count = choices.shape
    ordered = jnp.transpose(choices)
    live = jnp.transpose(used_mask)
    expert_range = jnp.arange(EXPERTS, dtype=jnp.int32)
    onehot = (ordered[:, :, None] == expert_range).astype(jnp.int32) * live[:, :, None]
    flat_hot = onehot.reshape(row_count * choice_count, EXPERTS)
    before = jnp.cumsum(flat_hot, axis=0) - flat_hot
    slot_index = lax.optimization_barrier(jnp.sum(before * flat_hot, axis=1)).reshape(choice_count, row_count)
    kept_mask = live * (slot_index < CAPACITY).astype(jnp.int32)
    slot_place = ordered * CAPACITY + jnp.minimum(slot_index, CAPACITY - 1)
    return (kept_mask, slot_place)

def to_blocks(values):
    rest = values.shape[2:]
    shaped = values.reshape((N_EP, SEG_ROWS, N_IMG, IMG_GROUP) + rest)
    shaped = jnp.swapaxes(shaped, 1, 2)
    return shaped.reshape((N_EP * N_IMG, SEG_ROWS * IMG_GROUP) + rest)

def from_blocks(values):
    rest = values.shape[2:]
    shaped = values.reshape((N_EP, N_IMG, SEG_ROWS, IMG_GROUP) + rest)
    shaped = jnp.swapaxes(shaped, 1, 2)
    return shaped.reshape((GRID, IMAGES) + rest)

def image_attention(packed):
    queries, key_rows, value_rows, key_ok = packed
    scores = jnp.einsum('shd,thd->hst', queries, key_rows, precision=highest) * HD ** (-0.5)
    scores = jnp.where(key_ok[None, None, :], scores, masked_score)
    scores = low_back(scores)
    probs = low(softmax_rows(scores))
    return jnp.einsum('hst,thd->shd', probs, value_rows, precision=highest)

def expert_apply(packed):
    expert_rows, weight_in, weight_out = packed
    pre_act = low_back(jnp.dot(expert_rows, weight_in, precision=highest))
    act = low(jax.nn.gelu(pre_act, approximate=False))
    return low_back(low(jnp.dot(act, weight_out, precision=highest)))

def fill_slots(rows, places, kept):
    terms = rows[None, :, :] * kept[:, :, None].astype(jnp.float32)
    empty = jnp.zeros((EXPERTS * CAPACITY, rows.shape[1]), jnp.float32)
    return empty.at[places.reshape(-1)].add(terms.reshape(-1, rows.shape[1]))

def pick_rows(table, places):
    return table[places]

def block_forward(tokens, gains, shifts, qkv_weight, out_weight, router_weight, w_in, w_out, valid, task_ids, top_counts, expert_ids):
    model_width = tokens.shape[2]
    block_count = N_EP * N_IMG
    normed_first = low(layer_norm(tokens, gains[0], shifts[0]))
    qkv_all = low_back(low(jnp.einsum('sid,de->sie', normed_first, qkv_weight, precision=highest)))
    split = qkv_all.reshape(GRID, IMAGES, 3, HEADS, HD)
    moved = jnp.transpose(split, (2, 1, 0, 3, 4))
    key_ok = jnp.transpose(valid) > 0
    attended = lax.map(jax.checkpoint(image_attention), (moved[0], moved[1], moved[2], key_ok))
    attended = jnp.transpose(attended, (1, 0, 2, 3)).reshape(GRID, IMAGES, model_width)
    attended = low_back(low(attended))
    branch = low_back(jnp.einsum('sid,de->sie', attended, out_weight, precision=highest))
    residual = tokens + branch
    normed_second = low(layer_norm(residual, gains[1], shifts[1]))
    task_router = router_weight[task_ids]
    logits = low_back(jnp.einsum('sid,ide->sie', normed_second, task_router, precision=highest))
    router_probs = softmax_rows(logits)
    expert_range = jnp.arange(EXPERTS, dtype=jnp.int32)
    chosen = expert_ids[..., None] == expert_range
    gate_probs = lax.optimization_barrier(jnp.sum(jnp.where(chosen, router_probs[:, :, None, :], 0.0), axis=-1))
    counts = top_counts[task_ids]
    used_mask = ((valid[:, :, None] > 0) & (jnp.arange(TOP_MAX, dtype=jnp.int32)[None, None, :] < counts[None, :, None])).astype(jnp.int32)
    kept_mask, slot_place = jax.vmap(route_slots)(to_blocks(expert_ids), to_blocks(used_mask))
    mix_weight = jnp.transpose(to_blocks(gate_probs), (0, 2, 1)) * kept_mask.astype(jnp.float32)
    row_blocks = to_blocks(normed_second)
    slots = low_back(jax.vmap(fill_slots)(row_blocks, slot_place, kept_mask))
    expert_in = jnp.transpose(slots.reshape(block_count, EXPERTS, CAPACITY, model_width), (1, 0, 2, 3))
    expert_in = expert_in.reshape(EXPERTS, block_count * CAPACITY, model_width)
    expert_res = lax.map(jax.checkpoint(expert_apply), (expert_in, w_in, w_out))
    expert_res = jnp.transpose(expert_res.reshape(EXPERTS, block_count, CAPACITY, model_width), (1, 0, 2, 3))
    expert_res = expert_res.reshape(block_count, EXPERTS * CAPACITY, model_width)
    picked = jax.vmap(pick_rows)(expert_res, slot_place)
    mixed_rows = lax.optimization_barrier(jnp.sum(picked * mix_weight[..., None], axis=1))
    return residual + from_blocks(mixed_rows)

def reference(tokens, cotangent, valid, task_ids, top_counts, expert_ids, gains, shifts, qkv_weight, out_weight, router_weight, w_in, w_out):
    floats = (tokens.astype(jnp.float32), gains.astype(jnp.float32), shifts.astype(jnp.float32), qkv_weight.astype(jnp.float32), out_weight.astype(jnp.float32), router_weight.astype(jnp.float32), w_in.astype(jnp.float32), w_out.astype(jnp.float32))

    def forward(token_f, gain_f, shift_f, qkv_f, out_f, router_f, w_in_f, w_out_f):
        return block_forward(token_f, gain_f, shift_f, qkv_f, out_f, router_f, w_in_f, w_out_f, valid, task_ids, top_counts, expert_ids)
    output, pullback = jax.vjp(forward, *floats)
    grads = pullback(cotangent.astype(jnp.float32))
    return (output.astype(jnp.bfloat16), grads[0], grads[1], grads[2], grads[3], grads[4], grads[5], grads[6], grads[7])
```

```python
import functools

import jax
import jax.numpy as jnp
from jax import lax
from jax.experimental import pallas as pl
from jax.experimental.pallas import tpu as pltpu
from jax.sharding import PartitionSpec as P

HD = 64
CAPACITY = 32
NORM_EPS = 1e-6
MASKED = -1e30
INTERPRET = False

F32 = jnp.float32
BF = jnp.bfloat16
I32 = jnp.int32


def shape(dims, dtype):
    return jax.ShapeDtypeStruct(dims, dtype)


def dot(a, b, ca, cb):
    return lax.dot_general(a, b, (((ca,), (cb,)), ((), ())), preferred_element_type=F32)


def nn(a, b):
    return dot(a, b, 1, 0)


def nt(a, b):
    return dot(a, b, 1, 1)


def tn(a, b):
    return dot(a, b, 0, 0)


def iota(dims, axis):
    return lax.broadcasted_iota(I32, dims, axis)


def col_sum(v):
    return jnp.sum(v, axis=0, keepdims=True)


def row_sum(v):
    return jnp.sum(v, axis=1, keepdims=True)


VMEM = pl.BlockSpec(memory_space=pltpu.VMEM)
SMEM = pl.BlockSpec(memory_space=pltpu.SMEM)
ANY = pl.BlockSpec(memory_space=pl.ANY)


def call(body, outs, args, scalars=0, scratch=(), name=None, flops=0, moved=0, exps=0):
    return pl.pallas_call(
        body,
        out_shape=outs,
        in_specs=[SMEM] * scalars + [VMEM] * (len(args) - scalars),
        out_specs=jax.tree.map(lambda _: VMEM, outs),
        scratch_shapes=list(scratch),
        compiler_params=pltpu.CompilerParams(vmem_limit_bytes=60 << 20),
        cost_estimate=pl.CostEstimate(flops=flops, bytes_accessed=moved, transcendentals=exps),
        name=name,
        interpret=INTERPRET,
    )(*args)


def pack_body(T, J, qkv, outw, router, norms, piece):
    rows, width = qkv.shape
    own = outw.shape[1]
    cat = jnp.concatenate([qkv[...].astype(F32), outw[...].astype(F32)], axis=1)
    for t in range((width + own) // 128):
        piece[t * rows : (t + 1) * rows, :] = cat[:, t * 128 : (t + 1) * 128].astype(BF)
    base = rows * ((width + own) // 128)
    piece[base : base + 16, :] = jnp.zeros((16, 128), BF)
    piece[base : base + T * J, : router.shape[1]] = router[...]
    piece[base + 8 : base + 12, : norms.shape[1]] = norms[...]


def unpack_body(n, zn, D, T, J, pos, *refs):
    pieces = refs[: 2 * n]
    wqkv, wout, rT, gs, grid_w, acc = refs[2 * n :]
    rows = D // (2 * zn)
    wide = 3 * D // n
    thin = D // n
    tiles = (wide + thin) // 128
    base = rows * tiles
    ep, z, c = pos[0], pos[1], pos[2]
    for cc in range(2):
        for k in range(n):
            for zz in range(zn):
                img = (z ^ zz) * 2 + (c ^ cc)
                start = pl.multiple_of(img * rows, 16)
                for t in range(tiles):
                    grid_w[ep ^ k, pl.ds(start, rows), t * 128 : (t + 1) * 128] = pieces[
                        cc * n + k
                    ][zz, t * rows : (t + 1) * rows, :]
    parts = [grid_w[e].astype(F32) for e in range(n)]
    wqkv[...] = jnp.concatenate([p[:, :wide] for p in parts], axis=1).astype(BF)
    wout[...] = jnp.concatenate([p[:, wide : wide + thin] for p in parts], axis=1).astype(BF)
    lanes = iota((128, D), 1)
    subs = iota((128, D), 0)
    total = jnp.zeros((16 * n, D), F32)
    for cc in range(2):
        for zz in range(zn):
            img = (z ^ zz) * 2 + (c ^ cc)
            sel = ((lanes == subs + img * rows) & (subs < rows)).astype(BF)
            tile = jnp.concatenate([pieces[cc * n + k][zz, base : base + 16, :] for k in range(n)], axis=0)
            total = total + nn(tile, sel)
    acc[...] = total
    for k in range(n):
        rT[pl.ds(pl.multiple_of((ep ^ k) * 8, 8), 8), :] = acc[16 * k : 16 * k + 8, :]
    norm = jnp.zeros((16, D), F32)
    for k in range(n):
        sel = ((lanes == subs + (ep ^ k) * thin) & (subs < thin)).astype(BF)
        norm = norm + nn(pieces[k][0, base : base + 16, :], sel)
    gs[...] = norm[8:16, :]


def route_body(S, I, TOP, E, ids_col, ids_row, place_col, place_row):
    R = S * I

    def order(v):
        return v if I == 1 else lax.rem(v, S) * I + lax.div(v, S)

    a = order(iota((R, R), 0))
    b = order(iota((R, R), 1))
    lower = (b < a).astype(F32).astype(BF)
    upper = (a < b).astype(F32).astype(BF)
    lane = iota((R, 128), 1)
    sub = iota((E, R), 0)
    base_c = jnp.zeros((1, 128), F32)
    base_r = jnp.zeros((E, 1), F32)
    found_c = jnp.full((R, 128), -1, I32)
    for j in range(TOP):
        ident = ids_col[:, j : j + 1]
        hot = (ident == lane).astype(F32)
        rank = row_sum((nn(lower, hot.astype(BF)) + base_c) * hot).astype(I32)
        base_c = base_c + col_sum(hot)
        kept = (rank < CAPACITY) & (ident >= 0)
        place = jnp.where(kept, ident * CAPACITY + rank, -1)
        found_c = jnp.where(lane == j, place, found_c)
        ident = ids_row[j : j + 1, :]
        hot = (ident == sub).astype(F32)
        rank = col_sum((nn(hot.astype(BF), upper) + base_r) * hot).astype(I32)
        base_r = base_r + row_sum(hot)
        kept = (rank < CAPACITY) & (ident >= 0)
        place_row[j : j + 1, :] = jnp.where(kept, ident * CAPACITY + rank, -1)
    place_col[...] = found_c


def normed(x):
    centre = jnp.mean(x, axis=1, keepdims=True)
    centred = x - centre
    scale = lax.rsqrt(jnp.mean(centred * centred, axis=1, keepdims=True) + NORM_EPS)
    return centred * scale, scale


def softmax(v, axis):
    e = jnp.exp(v - jnp.max(v, axis=axis, keepdims=True))
    return e / jnp.sum(e, axis=axis, keepdims=True)


def half_mask(rows, which):
    lane = iota((rows, 2 * HD), 1)
    return (lane < HD) if which == 0 else (lane >= HD)


def front_body(n, S, I, TOP, slots, *refs):
    toks = refs[:n]
    (cot, bias_row, tbias_c, tbias_r, ids_r, place_r, wqkv, wout, rT, gs) = refs[n : n + 10]
    outs = refs[n + 10 :]
    parts = outs[:n]
    qkv, n2_o, r_o, att_o, lse_o, probs_o, att_s, pay_s = outs[n:]
    D = wout.shape[0]
    R = S * I
    gains = gs[...]
    w = wqkv[...]
    for i in range(I):
        for k in range(n):
            x = toks[k][i].astype(F32)
            hat, _ = normed(x)
            n1 = (hat * gains[0:1] + gains[2:3]).astype(BF)
            qkv[i, k * S : (k + 1) * S, :] = nn(n1, w).astype(BF)
        lse = jnp.zeros((S, 128), F32)
        lane = iota((S, 128), 1)
        bias = bias_row[i : i + 1, :]
        for pair in range(D // (2 * HD)):
            at = pair * 2 * HD
            q = qkv[i, :S, at : at + 2 * HD].astype(F32) * HD ** (-0.5)
            keys = qkv[i, :, D + at : D + at + 2 * HD]
            vals = qkv[i, :, 2 * D + at : 2 * D + at + 2 * HD]
            mixed = None
            for h in range(2):
                mask = half_mask(S, h)
                s = nt(jnp.where(mask, q, 0.0).astype(BF), keys) + bias
                top = jnp.max(s, axis=1, keepdims=True)
                e = jnp.exp(s - top)
                total = row_sum(e)
                got = nn(e.astype(BF), vals) / total
                mixed = got if h == 0 else jnp.where(mask, got, mixed)
                lse = jnp.where(lane == pair * 2 + h, top + jnp.log(total), lse)
            att_s[i * S : (i + 1) * S, at : at + 2 * HD] = mixed
        lse_o[i * S : (i + 1) * S, :] = lse
    att = att_s[...]
    att_o[...] = att
    own = jnp.concatenate([toks[0][i] for i in range(I)], axis=0).astype(F32)
    r = own + nn(att.astype(BF), wout[...])
    r_o[...] = r
    hat, _ = normed(r)
    n2 = (hat * gains[1:2] + gains[3:4]).astype(BF)
    n2_o[...] = n2
    router = rT[...].astype(BF)
    probs_o[...] = softmax(nt(n2, router) + tbias_c[...], 1)
    probs_r = softmax(nt(router, n2) + tbias_r[...], 0)
    sub = iota((slots, R), 0)
    lsub = iota(probs_r.shape, 0)
    send = jnp.zeros((slots, R), F32)
    mix = jnp.zeros((slots, R), F32)
    for j in range(TOP):
        gate = col_sum(jnp.where(lsub == ids_r[j : j + 1, :], probs_r, 0.0))
        hot = sub == place_r[j : j + 1, :]
        send = jnp.where(hot, 1.0, send)
        mix = jnp.where(hot, gate, mix)
    weight = row_sum(mix)
    send = send.astype(BF)
    pay_s[:, :D] = nn(send, n2).astype(BF)
    pay_s[:, D:] = (nn(send, cot[...]) * weight).astype(BF)
    step = slots // n
    for k in range(n):
        parts[k][...] = pay_s[k * step : (k + 1) * step, :]


def tail_terms(u):
    z = jnp.abs(u)
    t = 1.0 / (1.0 + z * (0.3275911 * 0.7071067811865476))
    bell = jnp.exp(u * u * -0.5)
    poly = t * (
        0.254829592 * 0.5
        + t * (-0.284496736 * 0.5 + t * (1.421413741 * 0.5 + t * (-1.453152027 * 0.5 + t * (1.061405429 * 0.5))))
    )
    tail = poly * bell
    return jnp.where(u >= 0.0, 1.0 - tail, tail), bell * 0.3989422804014327


def expert_body(n, D, *refs):
    ins = refs[:n]
    w1, w2 = refs[n : n + 2]
    outs = refs[n + 2 : 2 * n + 2]
    h_s, d_s, ha_s, dh_s = refs[2 * n + 2 :]
    j = pl.program_id(0)
    rows = pl.ds(pl.multiple_of(j * CAPACITY, CAPACITY), CAPACITY)
    x = jnp.concatenate([r[rows, :D] for r in ins], axis=0)
    d = jnp.concatenate([r[rows, D:] for r in ins], axis=0)
    h_s[...] = nn(x, w1[0])
    d_s[...] = nt(d, w2[0])
    count, FF = h_s.shape
    cols = 512

    def step(i, _):
        at = pl.ds(pl.multiple_of(i * 16, 16), 16)
        for f in range(FF // cols):
            sl = slice(f * cols, (f + 1) * cols)
            u = h_s[at, sl]
            big, bell = tail_terms(u)
            ha_s[at, sl] = (u * big).astype(BF)
            dh_s[at, sl] = (d_s[at, sl] * (big + u * bell)).astype(BF)
        return 0

    lax.fori_loop(0, count // 16, step, 0)
    eo = nn(ha_s[...], w2[0]).astype(BF)
    ds = nt(dh_s[...], w1[0]).astype(BF)
    for k in range(n):
        outs[k][rows, :D] = eo[k * CAPACITY : (k + 1) * CAPACITY]
        outs[k][rows, D:] = ds[k * CAPACITY : (k + 1) * CAPACITY]


def experts(ins, w_in, w_out):
    J, D, FF = w_in.shape
    n = len(ins)
    count = n * CAPACITY
    whole = pl.BlockSpec(ins[0].shape, lambda j: (0, 0))
    return pl.pallas_call(
        functools.partial(expert_body, n, D),
        grid=(J,),
        in_specs=[whole] * n
        + [pl.BlockSpec((1, D, FF), lambda j: (j, 0, 0)), pl.BlockSpec((1, FF, D), lambda j: (j, 0, 0))],
        out_specs=[whole] * n,
        out_shape=[shape(a.shape, BF) for a in ins],
        scratch_shapes=[
            pltpu.VMEM((count, FF), F32),
            pltpu.VMEM((count, FF), F32),
            pltpu.VMEM((count, FF), BF),
            pltpu.VMEM((count, FF), BF),
        ],
        compiler_params=pltpu.CompilerParams(vmem_limit_bytes=60 << 20),
        cost_estimate=pl.CostEstimate(
            flops=8 * J * count * D * FF, bytes_accessed=4 * J * D * FF, transcendentals=J * count * FF
        ),
        name="experts",
        interpret=INTERPRET,
    )(*ins, w_in, w_out)


def wgrad_body(zn, JE, n, D, FT, fast, pos, *refs):
    if fast:
        own, e1, o1, o2, e2, e3, w1, w2 = refs[:8]
        refs = refs[8:]
    else:
        src, w1, w2 = refs[:3]
        refs = refs[3:]
    g1_o, g2_o, f1_o, f2_o, buf, h_s, d_s, ha_s, dh_s, sem = refs
    je, f = pl.program_id(0), pl.program_id(1)
    z, c = pos[0], pos[1]

    @pl.when((je == 0) & (f == 0))
    def _():
        if fast:
            table = [
                [own, e1, e2, e3],
                [e1, own, o1, o2],
                [o2, o1, own, e1],
                [e3, e2, e1, own],
            ]
            for zz in range(4):

                @pl.when(z == zz)
                def _():
                    for s in range(4):
                        for cc in range(2):
                            for q in range(JE):
                                pltpu.make_async_copy(
                                    table[zz][s].at[cc, :, q], buf.at[q, s, cc ^ c], sem.at[s, cc, q]
                                ).start()

            for s in range(4):
                for cc in range(2):
                    for q in range(JE):
                        pltpu.make_async_copy(own.at[0, :, 0], buf.at[q, s, 0], sem.at[s, cc, q]).wait()
        else:
            for s in range(zn):
                for cc in range(2):
                    for q in range(JE):
                        pltpu.make_async_copy(src.at[s, cc, :, q], buf.at[q, s, cc], sem.at[s, cc, q]).start()
            for s in range(zn):
                for cc in range(2):
                    for q in range(JE):
                        pltpu.make_async_copy(src.at[s, cc, :, q], buf.at[q, s, cc], sem.at[s, cc, q]).wait()

    rows = zn * 2 * n * CAPACITY
    block = buf[je].reshape(rows, 2 * D)
    x = block[:, :D]
    d = block[:, D:]
    w1t = jnp.transpose(w1[0])
    h_s[...] = nt(w1t, x)
    d_s[...] = nt(w2[0], d)
    cols = min(512, rows)

    def step(i, _):
        at = pl.ds(pl.multiple_of(i * 16, 16), 16)
        for b in range(rows // cols):
            sl = slice(b * cols, (b + 1) * cols)
            u = h_s[at, sl]
            big, bell = tail_terms(u)
            ha_s[at, sl] = (u * big).astype(BF)
            dh_s[at, sl] = (d_s[at, sl] * (big + u * bell)).astype(BF)
        return 0

    lax.fori_loop(0, FT // 16, step, 0)
    g2 = nn(ha_s[...], d).astype(BF)
    g1 = jnp.transpose(nn(dh_s[...], x)).astype(BF)
    g1_o[0] = g1
    g2_o[0] = g2
    f1_o[0] = g1.astype(F32)
    f2_o[0] = g2.astype(F32)


def weight_grads(sources, w_in, w_out, pos, JE, zn, n, fast):
    J, D, FF = w_in.shape
    rows = zn * 2 * n * CAPACITY
    FT = 512 if rows <= 2048 else 128
    grid_spec = pltpu.PrefetchScalarGridSpec(
        num_scalar_prefetch=1,
        grid=(JE, FF // FT),
        in_specs=[ANY] * len(sources)
        + [
            pl.BlockSpec((1, D, FT), lambda j, f, p: (j + p[2], 0, f)),
            pl.BlockSpec((1, FT, D), lambda j, f, p: (j + p[2], f, 0)),
        ],
        out_specs=[
            pl.BlockSpec((1, D, FT), lambda j, f, p: (j, 0, f)),
            pl.BlockSpec((1, FT, D), lambda j, f, p: (j, f, 0)),
            pl.BlockSpec((1, D, FT), lambda j, f, p: (j + p[2], 0, f)),
            pl.BlockSpec((1, FT, D), lambda j, f, p: (j + p[2], f, 0)),
        ],
        scratch_shapes=[
            pltpu.VMEM((JE, zn, 2, n, CAPACITY, 2 * D), BF),
            pltpu.VMEM((FT, rows), F32),
            pltpu.VMEM((FT, rows), F32),
            pltpu.VMEM((FT, rows), BF),
            pltpu.VMEM((FT, rows), BF),
            pltpu.SemaphoreType.DMA((zn, 2, JE)),
        ],
    )
    return pl.pallas_call(
        functools.partial(wgrad_body, zn, JE, n, D, FT, fast),
        grid_spec=grid_spec,
        out_shape=[
            shape((JE, D, FF), BF),
            shape((JE, FF, D), BF),
            shape((J, D, FF), F32),
            shape((J, FF, D), F32),
        ],
        compiler_params=pltpu.CompilerParams(vmem_limit_bytes=60 << 20),
        cost_estimate=pl.CostEstimate(
            flops=8 * JE * rows * D * FF, bytes_accessed=16 * JE * D * FF, transcendentals=JE * rows * FF
        ),
        name="weight_grads",
        interpret=INTERPRET,
    )(pos, *sources, w_in, w_out)


def widen_body(pos, a, b, fa, fb, oa, ob):
    oa[...] = a[...].astype(F32)
    ob[...] = b[...].astype(F32)


def widen(pos, a, b, fa, fb):
    JE, D, FF = a.shape
    grid_spec = pltpu.PrefetchScalarGridSpec(
        num_scalar_prefetch=1,
        grid=(JE, 3),
        in_specs=[
            pl.BlockSpec((1, D // 3, FF), lambda j, t, p: (j, t, 0)),
            pl.BlockSpec((1, FF // 3, D), lambda j, t, p: (j, t, 0)),
            ANY,
            ANY,
        ],
        out_specs=[
            pl.BlockSpec((1, D // 3, FF), lambda j, t, p: (j + p[3], t, 0)),
            pl.BlockSpec((1, FF // 3, D), lambda j, t, p: (j + p[3], t, 0)),
        ],
    )
    return pl.pallas_call(
        widen_body,
        grid_spec=grid_spec,
        out_shape=[shape(fa.shape, F32), shape(fb.shape, F32)],
        input_output_aliases={3: 0, 4: 1},
        compiler_params=pltpu.CompilerParams(vmem_limit_bytes=60 << 20),
        cost_estimate=pl.CostEstimate(flops=0, bytes_accessed=12 * JE * D * FF, transcendentals=0),
        name="widen",
        interpret=INTERPRET,
    )(pos, a, b, fa, fb)


def norm_back(grad, hat, scale, gain):
    g = grad * gain
    return scale * (g - jnp.mean(g, axis=1, keepdims=True) - hat * jnp.mean(g * hat, axis=1, keepdims=True))


def combine_body(n, TOP, slots, *refs):
    rets = refs[:n]
    (cot, place_c, ids_c, probs, r_i, n2, att, lse, wout, rT, gs) = refs[n : n + 11]
    out_o, dr_o, wire_o, delta_o, gout_o, grt_o, gn_o = refs[n + 11 :]
    R, D = r_i.shape
    lane = iota((R, slots), 1)
    p = probs[...]
    plane = iota(p.shape, 1)
    dy_low = cot[...]
    dy = dy_low.astype(F32)
    eo = jnp.concatenate([a[:, :D] for a in rets], axis=0)
    dslot = jnp.concatenate([a[:, D:] for a in rets], axis=0)
    inner = nt(dy_low, eo)
    send = jnp.zeros((R, slots), F32)
    mix = jnp.zeros((R, slots), F32)
    dprobs = jnp.zeros(p.shape, F32)
    for j in range(TOP):
        named = plane == ids_c[:, j : j + 1]
        gate = row_sum(jnp.where(named, p, 0.0))
        hot = lane == place_c[:, j : j + 1]
        send = jnp.where(hot, 1.0, send)
        mix = jnp.where(hot, gate, mix)
        dprobs = jnp.where(named, row_sum(jnp.where(hot, inner, 0.0)), dprobs)
    high = mix.astype(BF)
    low = (mix - high.astype(F32)).astype(BF)
    r = r_i[...]
    out_o[...] = (r + (nn(high, eo) + nn(low, eo))).astype(BF)
    dlogits = (p * (dprobs - row_sum(p * dprobs))).astype(BF)
    dn2 = nn(send.astype(BF), dslot) + nn(dlogits, rT[...].astype(BF))
    grt_o[...] = tn(dlogits, n2[...])
    hat, scale = normed(r)
    gn_o[0:1, :] = col_sum(dn2 * hat)
    gn_o[1:2, :] = col_sum(dn2)
    dr = dy + norm_back(dn2, hat, scale, gs[1:2, :])
    dr_o[...] = dr
    datt_out = dr.astype(BF)
    attended = att[...]
    gout_o[...] = tn(attended.astype(BF), datt_out)
    datt = nt(datt_out, wout[...]).astype(BF)
    wire_o[:R, :] = datt
    prod = datt.astype(F32) * attended
    stats = lse[...]
    slane = iota((R, 128), 1)
    delta = jnp.zeros((R, 128), F32)
    for pair in range(D // (2 * HD)):
        part = prod[:, pair * 2 * HD : (pair + 1) * 2 * HD]
        for h in range(2):
            total = row_sum(jnp.where(half_mask(R, h), part, 0.0))
            delta = jnp.where(slane == pair * 2 + h, total, delta)
    delta_o[...] = delta
    both = jnp.concatenate([jnp.transpose(stats)[:8], jnp.transpose(delta)[:8]], axis=0)
    high = both.astype(BF)
    low = (both - high.astype(F32)).astype(BF)
    wire_o[R : R + 16, :R] = high
    wire_o[R + 16 : R + 32, :R] = low
    if R < D:
        wire_o[R : R + 32, R:] = jnp.zeros((32, D - R), BF)


def dq_body(S, I, qkv, wire, lse, delta, bias_row, dq_o):
    D = dq_o.shape[1]
    for i in range(I):
        rows = slice(i * S, (i + 1) * S)
        bias = bias_row[i : i + 1, :]
        for pair in range(D // (2 * HD)):
            at = pair * 2 * HD
            q = qkv[i, :S, at : at + 2 * HD].astype(F32) * HD ** (-0.5)
            keys = qkv[i, :, D + at : D + at + 2 * HD]
            vals = qkv[i, :, 2 * D + at : 2 * D + at + 2 * HD]
            da = wire[rows, at : at + 2 * HD].astype(F32)
            mixed = None
            for h in range(2):
                mask = half_mask(S, h)
                lane = pair * 2 + h
                s = nt(jnp.where(mask, q, 0.0).astype(BF), keys) + bias
                p = jnp.exp(s - lse[rows, lane : lane + 1])
                dp = nt(jnp.where(mask, da, 0.0).astype(BF), vals)
                ds = (p * (dp - delta[rows, lane : lane + 1])).astype(BF)
                got = nn(ds, keys)
                mixed = got if h == 0 else jnp.where(mask, got, mixed)
            dq_o[rows, at : at + 2 * HD] = (mixed * HD ** (-0.5)).astype(BF)


def back_body(n, S, I, fast, pos, *refs):
    wires = refs[:n]
    (qkv, dq, tok, dr, bias_col, wqkv, gs, gout, grt, gn) = refs[n : n + 10]
    if fast:
        gtok_o, send_o, keep_o, q_s, d_s, dqkv_s = refs[n + 10 :]
    else:
        gtok_o, gqkv_o, gnorm_o, q_s, d_s, dqkv_s = refs[n + 10 :]
    D = dq.shape[1]
    R = S * I
    dqkv_s[:, :D] = dq[...]
    for i in range(I):
        rows = slice(i * S, (i + 1) * S)
        q_s[...] = (qkv[i, :, :D].astype(F32) * HD ** (-0.5)).astype(BF)
        for k in range(n):
            d_s[k * S : (k + 1) * S, :] = wires[k][rows, :]
        stats = jnp.concatenate(
            [
                wires[k][R : R + 16, rows].astype(F32) + wires[k][R + 16 : R + 32, rows].astype(F32)
                for k in range(n)
            ],
            axis=1,
        )
        bias = bias_col[rows, :]
        for pair in range(D // (2 * HD)):
            at = pair * 2 * HD
            keys = qkv[i, :S, D + at : D + at + 2 * HD].astype(F32)
            vals = qkv[i, :S, 2 * D + at : 2 * D + at + 2 * HD].astype(F32)
            qs = q_s[:, at : at + 2 * HD]
            ds_all = d_s[:, at : at + 2 * HD]
            mixed_k = None
            mixed_v = None
            for h in range(2):
                mask = half_mask(S, h)
                lane = pair * 2 + h
                s = nt(jnp.where(mask, keys, 0.0).astype(BF), qs) + bias
                p = jnp.exp(s - stats[lane : lane + 1, :])
                dp = nt(jnp.where(mask, vals, 0.0).astype(BF), ds_all)
                ds = (p * (dp - stats[8 + lane : 9 + lane, :])).astype(BF)
                got_k = nn(ds, qs)
                got_v = nn(p.astype(BF), ds_all)
                mixed_k = got_k if h == 0 else jnp.where(mask, got_k, mixed_k)
                mixed_v = got_v if h == 0 else jnp.where(mask, got_v, mixed_v)
            dqkv_s[rows, D + at : D + at + 2 * HD] = mixed_k.astype(BF)
            dqkv_s[rows, 2 * D + at : 2 * D + at + 2 * HD] = mixed_v.astype(BF)
    dqkv = dqkv_s[...]
    x = jnp.concatenate([tok[i] for i in range(I)], axis=0).astype(F32)
    hat, scale = normed(x)
    n1 = (hat * gs[0:1, :] + gs[2:3, :]).astype(BF)
    dn1 = nt(dqkv, wqkv[...])
    gtok_o[...] = dr[...] + norm_back(dn1, hat, scale, gs[0:1, :])
    norms = jnp.concatenate([col_sum(dn1 * hat), gn[0:1, :], col_sum(dn1), gn[1:2, :]], axis=0)
    gq = tn(n1, dqkv)
    if not fast:
        gqkv_o[...] = gq
        gnorm_o[...] = norms
        return
    c = pos[2]
    wide = 3 * D // n
    thin = D // n
    zn = D // (2 * (D // 8))
    per = D // (2 * zn)
    for e in range(n):
        block = jnp.concatenate([gq[:, e * wide : (e + 1) * wide], gout[:, e * thin : (e + 1) * thin]], axis=1)
        small = jnp.concatenate([grt[8 * e : 8 * e + 8, :], norms, jnp.zeros((4, D), F32)], axis=0)
        for zz in range(zn):
            a = block[(2 * zz) * per : (2 * zz + 1) * per]
            b = block[(2 * zz + 1) * per : (2 * zz + 2) * per]
            keep_o[e, zz * per : (zz + 1) * per, :] = jnp.where(c == 0, a, b)
            send_o[e, zz * per : (zz + 1) * per, :] = jnp.where(c == 0, b, a).astype(BF)
        keep_o[e, zn * per :, :] = small
        send_o[e, zn * per :, :] = small.astype(BF)


def add_core_body(n, pos, recv, keep, own_o, *sends):
    ep = pos[0]
    own_o[...] = keep[ep] + recv[ep].astype(F32)
    for k in range(1, n):
        sends[k - 1][...] = (keep[ep ^ k] + recv[ep ^ k].astype(F32)).astype(BF)


def add_ep_body(per, pos, own, a, b, c, keep_o, send_o, total):
    total[...] = own[...] + a[...].astype(F32) + b[...].astype(F32) + c[...].astype(F32)
    half = 2 * per
    high = pos[1] // 2
    keep_o[:half, :] = total[pl.ds(pl.multiple_of(high * half, 16), half), :]
    send_o[:half, :] = total[pl.ds(pl.multiple_of((1 - high) * half, 16), half), :].astype(BF)
    keep_o[half:, :] = total[2 * half :, :]
    send_o[half:, :] = total[2 * half :, :].astype(BF)


def add_z_body(per, pos, recv, keep, keep_o, send_o, total):
    total[...] = keep[...] + recv[...].astype(F32)
    low = lax.rem(pos[1], 2)
    keep_o[:per, :] = total[pl.ds(pl.multiple_of(low * per, 16), per), :]
    send_o[:per, :] = total[pl.ds(pl.multiple_of((1 - low) * per, 16), per), :].astype(BF)
    keep_o[per:, :] = total[2 * per :, :]
    send_o[per:, :] = total[2 * per :, :].astype(BF)


def add_last_body(per, wide, thin, pos, recv, keep, gq_o, go_o, small_o):
    total = keep[...] + recv[...].astype(F32)
    gq_o[...] = total[:per, :wide]
    go_o[...] = total[:per, wide : wide + thin]
    small_o[...] = total[per:, :]


def per_device(
    tokens, cotangent, valid, task_ids, top_counts, expert_ids, gains, shifts,
    qkv_weight, out_weight, router_weight, w_in, w_out,
):
    S, I, D = tokens.shape
    G = valid.shape[0]
    TOP = expert_ids.shape[2]
    T = router_weight.shape[0]
    J, _, FF = w_in.shape
    n = lax.axis_size("ep")
    m = lax.axis_size("img")
    zn = m // 2
    E = J * n
    R = S * I
    slots = E * CAPACITY
    ep = lax.axis_index("ep")
    img = lax.axis_index("img")
    z, c = img // 2, img % 2
    fast = n == 4 and m == 8 and J % 2 == 0 and I == 1

    if fast:

        def absolute(k):
            return ep ^ k

        def relative(v):
            return v ^ ep

        def hop(v, k):
            return lax.ppermute(v, "ep", [(i, i ^ k) for i in range(n)])

        fetch = hop

        def exchange(parts):
            return [parts[0]] + [hop(parts[k], k) for k in range(1, n)]

    else:

        def absolute(k):
            return (ep + k) % n

        def relative(v):
            return (v - ep + n) % n

        def fetch(v, k):
            return lax.ppermute(v, "ep", [(i, (i - k) % n) for i in range(n)])

        def exchange(parts):
            got = [lax.ppermute(parts[k], "ep", [(i, (i + k) % n) for i in range(n)]) for k in range(1, n)]
            return [parts[0]] + got[::-1]

    def core_swap(v):
        return lax.ppermute(v, "img", [(i, i ^ 1) for i in range(m)])

    def z_pair(v, k):
        return lax.ppermute(v, "img", [(i, i ^ (2 * k)) for i in range(m)])

    def z_even(v):
        return z_pair(v, 1)

    def z_odd(v):
        return lax.ppermute(v, "img", [(2, 4), (3, 5), (4, 2), (5, 3)])

    pos = jnp.stack([ep, z, c]).astype(I32)
    tok = jnp.transpose(tokens, (1, 0, 2))
    cot = jnp.transpose(cotangent, (1, 0, 2)).reshape(R, D)
    tok_all = [tok] + [fetch(tok, k) for k in range(1, n)]

    norms = jnp.concatenate([gains, shifts], axis=0)
    if fast:
        router_t = jnp.transpose(router_weight, (0, 2, 1)).reshape(T * J, router_weight.shape[1])
        per = D // m
        tiles = (3 * D // n + D // n) // 128
        piece = call(
            functools.partial(pack_body, T, J),
            shape((per * tiles + 16, 128), BF),
            (qkv_weight, out_weight, router_t, norms),
            name="pack",
        )[None]
        two = jnp.concatenate([piece, z_pair(piece, 1)], axis=0)
        four = jnp.concatenate([two, z_pair(two, 2)], axis=0)
        mine = [four] + [hop(four, k) for k in range(1, n)]
        other = [core_swap(v) for v in mine]
        wqkv, wout, rT, gs = call(
            functools.partial(unpack_body, n, zn, D, T, J),
            (shape((D, 3 * D), BF), shape((D, D), BF), shape((T * E, D), F32), shape((8, D), F32)),
            (pos, *mine, *other),
            scalars=1,
            scratch=[pltpu.VMEM((n, D, 4 * D // n), BF), pltpu.VMEM((16 * n, D), F32)],
            name="unpack",
        )
    else:
        rows_q = lax.all_gather(qkv_weight, "img", axis=0, tiled=True)
        rows_o = lax.all_gather(out_weight, "img", axis=0, tiled=True)
        rows_r = lax.all_gather(router_weight, "img", axis=1, tiled=True)
        wqkv = lax.all_gather(rows_q, "ep", axis=1, tiled=True)
        wout = lax.all_gather(rows_o, "ep", axis=1, tiled=True)
        router = lax.all_gather(rows_r, "ep", axis=2, tiled=True)
        rT = jnp.transpose(router.reshape(T, D, n, J), (2, 0, 3, 1)).reshape(T * E, D).astype(F32)
        gs = lax.all_gather(norms, "ep", axis=1, tiled=True).astype(F32)
        gs = jnp.concatenate([gs, jnp.zeros((4, D), F32)], axis=0)

    here = lax.dynamic_slice_in_dim(valid, ep * S, S, 0)
    here_i = jnp.transpose(here).reshape(R)
    blocks = jnp.transpose(valid).reshape(I, n, S)
    keys_ok = jnp.concatenate(
        [lax.dynamic_index_in_dim(blocks, absolute(k), 1, keepdims=False) for k in range(n)], axis=1
    )
    bias_row = jnp.where(keys_ok > 0, 0.0, MASKED).astype(F32)
    bias_col = jnp.where(here_i > 0, 0.0, MASKED).astype(F32)[:, None]
    task_row = jnp.repeat(task_ids, S)
    counts = jnp.sum(
        jnp.where(task_row[:, None] == jnp.arange(T, dtype=I32)[None, :], top_counts[None, :], 0), axis=1
    )
    chosen = jnp.transpose(expert_ids, (1, 0, 2)).reshape(R, TOP)
    used = (here_i[:, None] > 0) & (jnp.arange(TOP, dtype=I32)[None, :] < counts[:, None])
    ids_slot = jnp.where(used, relative(chosen // J) * J + chosen % J, -1)
    ids_gate = (chosen // J) * (T * J) + task_row[:, None] * J + chosen % J
    ids_gate_row = jnp.transpose(ids_gate)
    gate_task = (jnp.arange(T * E, dtype=I32) // J) % T
    other_task = gate_task[None, :] != task_row[:, None]
    tbias_c = jnp.where(other_task, MASKED, 0.0).astype(F32)
    tbias_r = jnp.transpose(tbias_c)
    place_c, place_r = call(
        functools.partial(route_body, S, I, TOP, E),
        (shape((R, 128), I32), shape((TOP, R), I32)),
        (ids_slot, jnp.transpose(ids_slot)),
        name="route",
    )

    step = slots // n
    front = call(
        functools.partial(front_body, n, S, I, TOP, slots),
        tuple(shape((step, 2 * D), BF) for _ in range(n))
        + (
            shape((I, n * S, 3 * D), BF),
            shape((R, D), BF),
            shape((R, D), F32),
            shape((R, D), F32),
            shape((R, 128), F32),
            shape((R, T * E), F32),
        ),
        (*tok_all, cot, bias_row, tbias_c, tbias_r, ids_gate_row, place_r, wqkv, wout, rT, gs),
        scratch=[pltpu.VMEM((R, D), F32), pltpu.VMEM((slots, 2 * D), BF)],
        name="front",
        flops=2 * I * n * S * D * 3 * D + 4 * R * n * S * D,
        moved=6 << 20,
        exps=R * n * S * 6,
    )
    parts = front[:n]
    qkv, n2, resid, att, lse, probs = front[n:]
    incoming = exchange(parts)
    returned = exchange(experts(incoming, w_in, w_out))

    if fast:
        JE = J // 2
        width = JE * CAPACITY
        mine = jnp.concatenate(
            [lax.dynamic_slice_in_dim(v, c * width, width, 0)[None] for v in incoming], axis=0
        )
        theirs = jnp.concatenate(
            [lax.dynamic_slice_in_dim(v, (1 - c) * width, width, 0)[None] for v in incoming], axis=0
        )
        block = jnp.stack([mine, core_swap(theirs)]).reshape(2, n, JE, CAPACITY, 2 * D)
        e1, o1 = z_even(block), z_odd(block)
        o2, e2 = z_odd(e1), z_even(o1)
        e3 = z_even(o2)
        wpos = jnp.stack([z, c, c * JE, (1 - c) * JE]).astype(I32)
        g1, g2, f1, f2 = weight_grads([block, e1, o1, o2, e2, e3], w_in, w_out, wpos, JE, zn, n, True)
        grad_w_in, grad_w_out = widen(wpos, core_swap(g1), core_swap(g2), f1, f2)
    else:
        block = jnp.stack(incoming).reshape(n, J, CAPACITY, 2 * D)
        everyone = lax.all_gather(block, "img", axis=0, tiled=False)
        everyone = everyone.reshape(zn, 2, n, J, CAPACITY, 2 * D)
        wpos = jnp.zeros((4,), I32)
        _, _, grad_w_in, grad_w_out = weight_grads([everyone], w_in, w_out, wpos, J, zn, n, False)

    output, dr, wire, delta, gout, grt, gn = call(
        functools.partial(combine_body, n, TOP, slots),
        (
            shape((R, D), BF),
            shape((R, D), F32),
            shape((R + 32, D), BF),
            shape((R, 128), F32),
            shape((D, D), F32),
            shape((T * E, D), F32),
            shape((2, D), F32),
        ),
        (*returned, cot, place_c, ids_gate, probs, resid, n2, att, lse, wout, rT, gs),
        name="combine",
        flops=8 * R * slots * D,
        moved=4 << 20,
    )
    wires = [wire] + [fetch(wire, k) for k in range(1, n)]
    dq = call(
        functools.partial(dq_body, S, I),
        shape((R, D), BF),
        (qkv, wire, lse, delta, bias_row),
        name="dq",
        flops=12 * R * n * S * D,
        moved=3 << 20,
        exps=R * n * S * 6,
    )
    back_args = (pos, *wires, qkv, dq, tok, dr, bias_col, wqkv, gs, gout, grt, gn)
    back_scratch = [pltpu.VMEM((n * S, D), BF), pltpu.VMEM((n * S, D), BF), pltpu.VMEM((R, 3 * D), BF)]
    back_cost = dict(flops=16 * R * n * S * D, moved=5 << 20, exps=R * n * S * 6)
    if fast:
        wide, thin = 3 * D // n, D // n
        gtok, send, keep = call(
            functools.partial(back_body, n, S, I, True),
            (shape((R, D), F32), shape((n, zn * per + 16, D), BF), shape((n, zn * per + 16, D), F32)),
            back_args,
            scalars=1,
            scratch=back_scratch,
            name="back",
            **back_cost,
        )
        rows = zn * per + 16
        added = call(
            functools.partial(add_core_body, n),
            (shape((rows, D), F32),) + tuple(shape((rows, D), BF) for _ in range(n - 1)),
            (pos, core_swap(send), keep),
            scalars=1,
            name="add_core",
        )
        keep, send = call(
            functools.partial(add_ep_body, per),
            (shape((2 * per + 16, D), F32), shape((2 * per + 16, D), BF)),
            (pos, added[0], *[hop(added[k], k) for k in range(1, n)]),
            scalars=1,
            scratch=[pltpu.VMEM((rows, D), F32)],
            name="add_ep",
        )
        keep, send = call(
            functools.partial(add_z_body, per),
            (shape((per + 16, D), F32), shape((per + 16, D), BF)),
            (pos, z_pair(send, 2), keep),
            scalars=1,
            scratch=[pltpu.VMEM((2 * per + 16, D), F32)],
            name="add_z",
        )
        grad_qkv, grad_out, small = call(
            functools.partial(add_last_body, per, wide, thin),
            (shape((per, wide), F32), shape((per, thin), F32), shape((16, D), F32)),
            (pos, z_pair(send, 1), keep),
            scalars=1,
            name="add_last",
        )
        mine = lax.dynamic_slice_in_dim(small[: T * J], img * per, per, 1)
        grad_router = jnp.transpose(mine.reshape(T, J, per), (0, 2, 1))
        norm_grads = lax.dynamic_slice_in_dim(small[8:12], ep * thin, thin, 1)
        grad_gains, grad_shifts = norm_grads[:2], norm_grads[2:]
    else:
        gtok, gqkv, gnorm = call(
            functools.partial(back_body, n, S, I, False),
            (shape((R, D), F32), shape((D, 3 * D), F32), shape((4, D), F32)),
            back_args,
            scalars=1,
            scratch=back_scratch,
            name="back",
            **back_cost,
        )
        grad_r = jnp.transpose(grt.reshape(n, T, J, D), (1, 3, 0, 2)).reshape(T, D, E)

        def scatter(v, axis, dim):
            return lax.psum_scatter(v.astype(BF), axis, scatter_dimension=dim, tiled=True).astype(F32)

        grad_qkv = scatter(scatter(gqkv, "ep", 1), "img", 0)
        grad_out = scatter(scatter(gout, "ep", 1), "img", 0)
        grad_router = scatter(scatter(grad_r, "ep", 2), "img", 1)
        norm_grads = lax.psum(scatter(gnorm, "ep", 1).astype(BF), "img").astype(F32)
        grad_gains, grad_shifts = norm_grads[:2], norm_grads[2:]

    def as_cells(v):
        return jnp.transpose(v.reshape(I, S, D), (1, 0, 2))

    return (
        as_cells(output),
        as_cells(gtok),
        grad_gains,
        grad_shifts,
        grad_qkv,
        grad_out,
        grad_router,
        grad_w_in,
        grad_w_out,
    )


def solution(mesh):
    cells = P("ep", "img", None)
    return jax.shard_map(
        per_device,
        mesh=mesh,
        in_specs=(
            cells,
            cells,
            P(None, "img"),
            P("img"),
            P(),
            cells,
            P(None, "ep"),
            P(None, "ep"),
            P("img", "ep"),
            P("img", "ep"),
            P(None, "img", "ep"),
            P("ep", None, None),
            P("ep", None, None),
        ),
        out_specs=(
            cells,
            cells,
            P(None, "ep"),
            P(None, "ep"),
            P("img", "ep"),
            P("img", "ep"),
            P(None, "img", "ep"),
            P("ep", None, None),
            P("ep", None, None),
        ),
        check_vma=False,
    )
```
